32 devices in a mesh: chan: 8 (over y, x, core), tm: 4 (over z).
Axes of the slice: x: 2, y: 2, z: 4, core: 2. Of those that a mesh axis runs over, the one named last changes fastest.
Arguments:
- records: float32 [2560, 4, 7936], P('chan', 'tm'), may hold values from -6 to 6
- offsets: int32 [4], P('tm'), may hold values from 0 to 256
Outputs:
- correlations: float32 [2, 640, 2, 20480], P(None, 'tm', None, 'chan')
The draws below stay inside these ranges and needn't reach their ends.
All inputs are finite; a program needn't handle non-finite values.
Results may differ from the reference program's by a relative error of at most 0.0001.
Values sent between devices are 32-bit elements; how exact they have to be, the bound alone decides.
A program may use at most 128 MiB of HBM per device.

```python
import jax
import jax.numpy as jnp
from jax import lax

CB = 320
SRC = 8
LEN = 7680
SLACK = 256
FB = 640
FLO = 64
SMOOTH = 64
ROUNDS = 2
SEG = 7936
CHANNELS = 2560
WINDOWS = 4
N_CHAN = 8


def draw_offsets(key, part):
    values = jax.random.randint(key, (WINDOWS,), 0, SLACK + 1)
    chosen = jax.random.randint(jax.random.fold_in(key, 11), (), 0, WINDOWS)
    values = values.at[chosen].set(SLACK)
    values = values.at[(chosen + 1) % WINDOWS].set(0)
    return values.astype(jnp.int32)


def level_of(stream_key, dims, shards, smallest, top_value):
    gain, own = 1.0, jax.random.fold_in(stream_key, 6)
    for position, blocks in shards:
        steps = jnp.exp(jax.random.uniform(jax.random.fold_in(own, position), (blocks,), jnp.float32, smallest / len(shards), top_value / len(shards)))
        gain = gain * jnp.repeat(steps, dims[position] // blocks).reshape([-1 if axis == position else 1 for axis in range(len(dims))])
    return gain


def centred(key, dims, scale, limit, pieces=(), kind=jnp.bfloat16):
    result = scale * jax.random.normal(key, dims, jnp.float32)
    if pieces:
        result = result * level_of(key, dims, pieces, -0.22, 0.18)
    return jnp.clip(result, -limit, limit).astype(kind)


def setup_inputs(seed: int = 0) -> dict:
    keys = jax.random.split(jax.random.key(seed), 3)
    records = centred(keys[0], (CHANNELS, WINDOWS, SEG), 1.0, 6.0, ((0, 8), (1, 4)), jnp.float32)
    offsets = draw_offsets(jax.random.fold_in(keys[2], 71), 0)
    return {"records": records, "offsets": offsets}


def whiten_block(block, offsets):

    def cut(rec, off):
        return lax.dynamic_slice_in_dim(rec, off, LEN, 1)
    windows = jax.vmap(cut, in_axes=(1, 0), out_axes=1)(block, offsets.astype(jnp.int32))
    spectrum = jnp.fft.rfft(windows, axis=-1)[..., FLO:FLO + FB]
    spec_re = jnp.real(spectrum)
    spec_im = jnp.imag(spectrum)
    amplitude = jnp.sqrt(spec_re * spec_re + spec_im * spec_im)
    bins = jnp.arange(FB)
    kernel = (jnp.abs(bins[:, None] - bins[None, :]) <= SMOOTH).astype(amplitude.dtype)
    counts = lax.optimization_barrier(jnp.sum(kernel, axis=0))
    smooth = jnp.einsum('cwk,kl->cwl', amplitude, kernel, precision=lax.Precision.HIGHEST) / counts
    scale = 1.0 / (smooth + 1e-06)
    return jnp.stack([spec_re * scale, spec_im * scale], axis=2)

def reference(records, offsets):
    blocks = records.reshape(N_CHAN, CB, WINDOWS, SEG)
    white = lax.map(lambda blk: whiten_block(blk, offsets), blocks)
    hp = lax.Precision.HIGHEST
    results = []
    for rnd in range(1, ROUNDS + 1):
        partner = jnp.roll(white, -rnd, axis=0)[:, :SRC]
        ar, ai = (white[:, :, :, 0], white[:, :, :, 1])
        br, bi = (partner[:, :, :, 0], partner[:, :, :, 1])
        real_part = jnp.einsum('biwf,bjwf->bfij', ar, br, precision=hp) + jnp.einsum('biwf,bjwf->bfij', ai, bi, precision=hp)
        imag_part = jnp.einsum('biwf,bjwf->bfij', ai, br, precision=hp) - jnp.einsum('biwf,bjwf->bfij', ar, bi, precision=hp)
        both = jnp.stack([real_part, imag_part], axis=2) / WINDOWS
        both = jnp.transpose(both, (1, 2, 0, 3, 4)).reshape(FB, 2, N_CHAN * CB * SRC)
        results.append(both)
    return jnp.stack(results, axis=0)
```

```python
import functools
import math

import jax
import jax.numpy as jnp
import numpy as np
from jax import lax
from jax.experimental import pallas as pl
from jax.experimental.pallas import tpu as pltpu
from jax.sharding import PartitionSpec as P

MESH = pl.DeviceIdType.MESH
SRC = 8
LEN = 7680
FB = 640
FLO = 64
SMOOTH = 64
ROUNDS = 2
M = 15
L = LEN // M
Q0 = FLO // M
NQ = 48
BASE = 16
START = BASE + M * Q0 - FLO
ROWS = START + M // 2 + M * (NQ - 1) + 5
LANES = 128
PARTS = LEN // LANES
CT = 64
WIDE = CT * SRC
KB = 40


def split(x):
    hi = x.astype(jnp.bfloat16)
    return hi, (x - hi.astype(jnp.float32)).astype(jnp.bfloat16)


def twice(x):
    return jnp.concatenate(split(x), 1)


def tables(n):
    a = np.arange(L)
    q = Q0 + np.arange(NQ)
    angle = 2.0 * math.pi * ((q[:, None] * a[None, :]) % L) / L
    full = np.concatenate([np.cos(angle), np.sin(angle)]).astype(np.float32)
    hi = full.astype(jnp.bfloat16)
    lo = (full - hi.astype(np.float32)).astype(jnp.bfloat16)
    both = np.concatenate([hi, lo])
    r = np.arange(1, M // 2 + 1)
    turn = 2.0 * math.pi * (r[:, None] * a[None, :]) / LEN
    twiddle = np.stack([np.cos(turn), np.sin(turn)], 1).reshape(2 * len(r), L)
    twiddle = np.repeat(twiddle[:, None, :], 8, 1).astype(np.float32)
    k = np.arange(FB)
    band = (np.abs(k[:, None] - k[None, :]) <= SMOOTH).astype(jnp.bfloat16)
    lane = np.arange(LANES)[:, None]
    col = np.arange(2 * WIDE)[None, :]
    spread = lane == (col // WIDE) * CT + (col % WIDE) // SRC
    spread = np.concatenate([spread, spread]).astype(jnp.bfloat16)
    packed = np.arange(pack_width(n))[:, None]
    col = np.arange(2 * n * LANES)[None, :]
    fan = packed == (col // LANES) * SRC + col % SRC
    fan = np.concatenate([fan, fan]).astype(jnp.bfloat16)
    return twiddle, both, band, spread, fan


def pack_width(n):
    return -(-2 * SRC * n // LANES) * LANES


C3 = math.sqrt(3.0) / 2.0
C51, C52 = math.cos(2 * math.pi / 5), math.cos(4 * math.pi / 5)
S51, S52 = math.sin(2 * math.pi / 5), math.sin(4 * math.pi / 5)


def dft3(x0, x1, x2):
    t = x1 + x2
    return x0 + t, x0 - 0.5 * t, C3 * (x2 - x1)


def dft5(x):
    t1, t2 = x[1] + x[4], x[2] + x[3]
    d1, d2 = x[1] - x[4], x[2] - x[3]
    re0 = x[0] + t1 + t2
    re1 = x[0] + C51 * t1 + C52 * t2
    re2 = x[0] + C52 * t1 + C51 * t2
    im1 = -(S51 * d1 + S52 * d2)
    im2 = S51 * d2 - S52 * d1
    return re0, re1, im1, re2, im2


def dft15(x):
    columns = [dft3(*[x[(5 * n1 + 3 * n2) % 15] for n1 in range(3)]) for n2 in range(5)]
    z = dft5([c[0] for c in columns])
    u = dft5([c[1] for c in columns])
    v = dft5([c[2] for c in columns])
    out = {}
    out[(0, 0)] = (z[0], None)
    out[(0, 1)] = (z[1], z[2])
    out[(0, 2)] = (z[3], z[4])
    out[(1, 0)] = (u[0], v[0])
    for j, (b, s) in ((1, (1, 2)), (2, (3, 4))):
        out[(1, j)] = (u[b] - v[s], u[s] + v[b])
        out[(1, 5 - j)] = (u[b] + v[s], v[b] - u[s])
    bins = [None] * 8
    for (k1, k2), (re, im) in out.items():
        k = (10 * k1 + 6 * k2) % 15
        if k <= 7:
            bins[k] = (re, im)
        else:
            bins[15 - k] = (re, -im)
    return bins


def first_stage(rows, base, off, x_ref, twiddle_ref, hi_ref, lo_ref):
    lane = lax.broadcasted_iota(jnp.int32, (16, LANES), 1)
    extra = rows - PARTS

    def put(row, c0, a0, value):
        hi, lo = split(value)
        hi_ref[pl.ds(row * CT + c0, 16), pl.ds(a0, LANES)] = hi
        lo_ref[pl.ds(row * CT + c0, 16), pl.ds(a0, LANES)] = lo

    def block(i, carry):
        c0 = pl.multiple_of(i * 16, 16)

        def load(j):
            return x_ref[pl.ds(base + c0 * rows + j, 16, stride=rows), :]

        for t in range(L // LANES):
            x = []
            for b in range(M):
                j = b * (L // LANES) + t
                value = load(j)
                if j < extra:
                    value = jnp.where(lane + j * LANES < off, load(j + PARTS), value)
                x.append(value)
            bins = dft15(x)
            a0 = t * LANES
            put(14, c0, a0, bins[0][0])
            for r in range(1, 8):
                re, im = bins[r]
                cos = twiddle_ref[2 * r - 2, :, a0 : a0 + LANES]
                sin = twiddle_ref[2 * r - 1, :, a0 : a0 + LANES]
                cos = jnp.concatenate([cos, cos], 0)
                sin = jnp.concatenate([sin, sin], 0)
                put(2 * r - 2, c0, a0, re * cos + im * sin)
                put(2 * r - 1, c0, a0, im * cos - re * sin)
        return carry

    lax.fori_loop(0, CT // 16, block, 0)


def second_stage(both_ref, hi_ref, lo_ref, w_ref):
    nt = (((1,), (1,)), ((), ()))
    low = lax.broadcasted_iota(jnp.int32, (NQ, LANES), 1) < CT

    def second(row, count):
        window = slice(row * CT, (row + count) * CT)
        p = lax.dot_general(both_ref[...], hi_ref[window, :], nt, preferred_element_type=jnp.float32)
        s = lax.dot_general(both_ref[: 2 * NQ, :], lo_ref[window, :], nt, preferred_element_type=jnp.float32)
        z = p[: 2 * NQ] + p[2 * NQ :] + s
        return z[:NQ], z[NQ:]

    for pair in range(4):
        zc, zs = second(4 * pair, min(4, M - 4 * pair))
        for i in range(2):
            r = 2 * pair + 1 + i
            if r == 8:
                w_ref[pl.ds(START, NQ, stride=M), :] = jnp.concatenate([zc[:, LANES:], -zs[:, LANES:]], 1)
                continue
            c = zc[:, i * LANES : (i + 1) * LANES]
            s = pltpu.roll(zs[:, i * LANES : (i + 1) * LANES], CT, 1)
            w_ref[pl.ds(START + r, NQ, stride=M), :] = c + jnp.where(low, s, -s)
            w_ref[pl.ds(START - r, NQ, stride=M), :] = jnp.where(low, c, -c) - s


def normalised(band_ref, w_ref):
    spec = w_ref[BASE : BASE + FB, :]
    power = spec * spec
    amp = jnp.sqrt(power + pltpu.roll(power, CT, 1))
    high = amp.astype(jnp.bfloat16).astype(jnp.float32)
    low = lax.broadcasted_iota(jnp.int32, (FB, LANES), 1) < CT
    parts = jnp.where(low, high, amp - high).astype(jnp.bfloat16)
    total = jnp.dot(band_ref[...], parts, preferred_element_type=jnp.float32)
    total = total + pltpu.roll(total, CT, 1)
    k = lax.broadcasted_iota(jnp.int32, (FB, LANES), 0)
    count = jnp.minimum(k + SMOOTH, FB - 1) - jnp.maximum(k - SMOOTH, 0) + 1
    count = count.astype(jnp.float32)
    return spec * (count / (total + 1e-06 * count))


def kernel(n, nc, rows, nt, off_ref, x_hbm, tw_hbm, both_hbm, band_hbm, spread_hbm, fan_hbm, o_hbm,
           x_ref, tw_ref, both_ref, band_ref, spread_ref, fan_ref, hi_ref, lo_ref, w_ref, white, recv,
           src_send, src_recv, b_ref, a_ref, stage,
           x_sem, const_sem, send_sem, recv_sem, ssend_sem, srecv_sem, out_sem):
    me = lax.axis_index("tm")
    blk = lax.axis_index("chan")
    bins = FB // n
    nsub = bins // KB
    off = off_ref[0]

    def fetch(t):
        part = pl.ds(t * CT * rows, CT * rows)
        return pltpu.make_async_copy(x_hbm.at[part, :], x_ref.at[part, :], x_sem.at[t])

    pairs = ((tw_hbm, tw_ref), (both_hbm, both_ref), (band_hbm, band_ref), (spread_hbm, spread_ref), (fan_hbm, fan_ref))
    consts = [pltpu.make_async_copy(src, dst, const_sem.at[i]) for i, (src, dst) in enumerate(pairs)]
    fetch(0).start()
    for c in consts[:3]:
        c.start()
    for t in range(1, nt):
        fetch(t).start()
    for c in consts[3:]:
        c.start()

    barrier = pltpu.get_barrier_semaphore()
    chan_steps = sorted({s % nc for r in range(1, ROUNDS + 1) for s in (r, -r)} - {0})
    for sh in range(1, n):
        pl.semaphore_signal(barrier, inc=1, device_id={"tm": lax.rem(me + sh, n)}, device_id_type=MESH)
    for s in chan_steps:
        pl.semaphore_signal(barrier, inc=1, device_id={"chan": lax.rem(blk + s, nc)}, device_id_type=MESH)

    def exchange(t, j, sh):
        peer = lax.rem(me + sh, n)
        return pltpu.make_async_remote_copy(
            src_ref=white.at[t, pl.ds(pl.multiple_of(peer * bins + j * KB, 8), KB), :],
            dst_ref=recv.at[sh - 1, t, pl.ds(pl.multiple_of(j * KB, 8), KB), :],
            send_sem=send_sem.at[t, sh - 1, j],
            recv_sem=recv_sem.at[t, sh - 1, j],
            device_id={"tm": peer},
            device_id_type=MESH,
        )

    order = list(range(2, n)) + [1]

    def transform(t, carry):
        fetch(t).wait()

        @pl.when(t == 0)
        def _():
            consts[0].wait()

        first_stage(rows, t * CT * rows, off, x_ref, tw_ref, hi_ref, lo_ref)

        @pl.when(t == 0)
        def _():
            consts[1].wait()

        second_stage(both_ref, hi_ref, lo_ref, w_ref)

        @pl.when(t == 0)
        def _():
            consts[2].wait()

        white[t] = normalised(band_ref, w_ref)

        @pl.when(t == 0)
        def _():
            pl.semaphore_wait(barrier, n - 1 + len(chan_steps))

        for j in range(nsub):
            for sh in order:
                exchange(t, j, sh).start()
        return carry

    lax.fori_loop(0, nt, transform, 0)

    mine = pl.multiple_of(me * bins, 8)
    for j in range(nsub):
        for sh in order:
            exchange(0, j, sh).wait_recv()
    lane = lax.broadcasted_iota(jnp.int32, (bins, LANES), 1)
    for tile in range(src_send.shape[1] // LANES):
        packed = jnp.zeros((bins, LANES), jnp.float32)
        for sh in range(n):
            at = sh * 2 * SRC - tile * LANES
            if not 0 <= at < LANES:
                continue
            value = white[0, pl.ds(mine, bins), :] if sh == 0 else recv[sh - 1, 0]
            re = pltpu.roll(value, at, 1) if at else value
            im = pltpu.roll(value, (at + SRC - CT) % LANES, 1)
            packed = jnp.where((lane >= at) & (lane < at + SRC), re, packed)
            packed = jnp.where((lane >= at + SRC) & (lane < at + 2 * SRC), im, packed)
        src_send[:, tile * LANES : (tile + 1) * LANES] = packed

    def source(r):
        return pltpu.make_async_remote_copy(
            src_ref=src_send,
            dst_ref=src_recv.at[r - 1],
            send_sem=ssend_sem.at[r - 1],
            recv_sem=srecv_sem.at[r - 1],
            device_id={"chan": lax.rem(blk + nc - r, nc)},
            device_id_type=MESH,
        )

    for r in range(1, ROUNDS + 1):
        source(r).start()
    for c in consts[3:]:
        c.wait()
    for r in range(1, ROUNDS + 1):
        source(r).wait_recv()
        b_ref[r - 1] = jnp.dot(twice(src_recv[r - 1]), fan_ref[...], preferred_element_type=jnp.float32) * (1.0 / n)

    def place(t, j, slot):
        return pltpu.make_async_copy(
            stage.at[slot],
            o_hbm.at[:, pl.ds(pl.multiple_of(j * KB, 8), KB), :, pl.ds(pl.multiple_of(t * WIDE, LANES), WIDE)],
            out_sem.at[slot],
        )

    def pairing(u, carry):
        t = lax.div(u, nsub)
        j = lax.rem(u, nsub)
        slot = lax.rem(u, 2)

        @pl.when(t > 0)
        def _():
            for sh in order:
                exchange(t, j, sh).wait_recv()

        k0 = pl.multiple_of(j * KB, 8)
        a = [white[t, pl.ds(pl.multiple_of(mine + k0, 8), KB), :]]
        a += [recv[sh - 1, t, pl.ds(k0, KB), :] for sh in range(1, n)]
        a_ref[...] = jnp.dot(twice(jnp.concatenate(a, 0)), spread_ref[...], preferred_element_type=jnp.float32)

        @pl.when(u >= 2)
        def _():
            place(t, j, slot).wait()

        def group(g, carry):
            g8 = pl.multiple_of(g * 8, 8)
            b = [[[b_ref[rnd, pl.ds(pl.multiple_of(k0 + g8, 8), 8), (2 * w + p) * LANES : (2 * w + p + 1) * LANES]
                   for p in range(2)] for w in range(n)] for rnd in range(ROUNDS)]
            for tile in range(WIDE // LANES):
                lanes = slice(tile * LANES, (tile + 1) * LANES)
                far = slice(WIDE + tile * LANES, WIDE + (tile + 1) * LANES)
                ar = [a_ref[pl.ds(w * KB + g8, 8), lanes] for w in range(n)]
                ai = [a_ref[pl.ds(w * KB + g8, 8), far] for w in range(n)]
                for rnd in range(ROUNDS):
                    real = imag = None
                    for w in range(n):
                        br, bi = b[rnd][w]
                        p = ar[w] * br + ai[w] * bi
                        q = ai[w] * br - ar[w] * bi
                        real = p if real is None else real + p
                        imag = q if imag is None else imag + q
                    stage[slot, rnd, pl.ds(g8, 8), 0, lanes] = real
                    stage[slot, rnd, pl.ds(g8, 8), 1, lanes] = imag
            return carry

        lax.fori_loop(0, KB // 8, group, 0)
        place(t, j, slot).start()
        return carry

    lax.fori_loop(0, nt * nsub, pairing, 0)

    for r in range(1, ROUNDS + 1):
        source(r).wait_send()

    def drain(t, carry):
        for j in range(nsub):
            for sh in order:
                exchange(t, j, sh).wait_send()
        return carry

    lax.fori_loop(0, nt, drain, 0)
    for u in range(nt * nsub - 2, nt * nsub):
        place(u // nsub, u % nsub, u % 2).wait()


def shards(records, offsets):
    chans = records.shape[0]
    n, nc = lax.axis_size("tm"), lax.axis_size("chan")
    rows = records.shape[2] // LANES
    nt = chans // CT
    bins = FB // n
    nsub = bins // KB
    assert records.shape[1] == 1 and chans % CT == 0 and bins % KB == 0
    flat = records.reshape(chans * rows, LANES)
    consts = [jnp.asarray(c) for c in tables(n)]
    anyspace = pl.BlockSpec(memory_space=pl.ANY)
    f32, bf16 = jnp.float32, jnp.bfloat16
    return pl.pallas_call(
        functools.partial(kernel, n, nc, rows, nt),
        in_specs=[pl.BlockSpec(memory_space=pltpu.SMEM)] + [anyspace] * 6,
        out_specs=anyspace,
        out_shape=jax.ShapeDtypeStruct((ROUNDS, bins, 2, chans * SRC), f32),
        scratch_shapes=[
            pltpu.VMEM((chans * rows, LANES), f32),
            *[pltpu.VMEM(c.shape, c.dtype) for c in consts],
            pltpu.VMEM((M * CT, L), bf16),
            pltpu.VMEM((M * CT, L), bf16),
            pltpu.VMEM((ROWS + 8, LANES), f32),
            pltpu.VMEM((nt, FB, LANES), f32),
            pltpu.VMEM((n - 1, nt, bins, LANES), f32),
            pltpu.VMEM((bins, pack_width(n)), f32),
            pltpu.VMEM((ROUNDS, bins, pack_width(n)), f32),
            pltpu.VMEM((ROUNDS, bins, 2 * n * LANES), f32),
            pltpu.VMEM((n * KB, 2 * WIDE), f32),
            pltpu.VMEM((2, ROUNDS, KB, 2, WIDE), f32),
            pltpu.SemaphoreType.DMA((nt,)),
            pltpu.SemaphoreType.DMA((5,)),
            pltpu.SemaphoreType.DMA((nt, n - 1, nsub)),
            pltpu.SemaphoreType.DMA((nt, n - 1, nsub)),
            pltpu.SemaphoreType.DMA((ROUNDS,)),
            pltpu.SemaphoreType.DMA((ROUNDS,)),
            pltpu.SemaphoreType.DMA((2,)),
        ],
        compiler_params=pltpu.CompilerParams(
            collective_id=0, has_side_effects=True, vmem_limit_bytes=60 << 20
        ),
        name="correlate",
    )(offsets, flat, *consts)


def solution(mesh):
    return jax.shard_map(
        shards,
        mesh=mesh,
        in_specs=(P("chan", "tm", None), P("tm")),
        out_specs=P(None, "tm", None, "chan"),
        check_vma=False,
    )
```

```python
import functools
import math

import jax
import jax.numpy as jnp
import numpy as np
from jax import lax
from jax.experimental import pallas as pl
from jax.experimental.pallas import tpu as pltpu
from jax.sharding import PartitionSpec as P

MESH = pl.DeviceIdType.MESH
SRC = 8
LEN = 7680
FB = 640
FLO = 64
SMOOTH = 64
ROUNDS = 2
M = 15
L = LEN // M
Q0 = FLO // M
NQ = 48
BASE = 16
START = BASE + M * Q0 - FLO
ROWS = START + M // 2 + M * (NQ - 1) + 5
LANES = 128
PARTS = LEN // LANES
CT = 64
WIDE = CT * SRC
KB = 40


def split(x):
    hi = x.astype(jnp.bfloat16)
    return hi, (x - hi.astype(jnp.float32)).astype(jnp.bfloat16)


def twice(x):
    return jnp.concatenate(split(x), 1)


def tables(n):
    a = np.arange(L)
    q = Q0 + np.arange(NQ)
    angle = 2.0 * math.pi * ((q[:, None] * a[None, :]) % L) / L
    full = np.concatenate([np.cos(angle), np.sin(angle)]).astype(np.float32)
    hi = full.astype(jnp.bfloat16)
    lo = (full - hi.astype(np.float32)).astype(jnp.bfloat16)
    both = np.concatenate([hi, lo])
    r = np.arange(1, M // 2 + 1)
    turn = 2.0 * math.pi * (r[:, None] * a[None, :]) / LEN
    twiddle = np.stack([np.cos(turn), np.sin(turn)], 1).reshape(2 * len(r), L)
    twiddle = np.repeat(twiddle[:, None, :], 8, 1).astype(np.float32)
    k = np.arange(FB)
    band = (np.abs(k[:, None] - k[None, :]) <= SMOOTH).astype(jnp.bfloat16)
    lane = np.arange(LANES)[:, None]
    col = np.arange(2 * WIDE)[None, :]
    spread = lane == (col // WIDE) * CT + (col % WIDE) // SRC
    spread = np.concatenate([spread, spread]).astype(jnp.bfloat16)
    packed = np.arange(pack_width(n))[:, None]
    col = np.arange(2 * n * LANES)[None, :]
    fan = packed == (col // LANES) * SRC + col % SRC
    fan = np.concatenate([fan, fan]).astype(jnp.bfloat16)
    return twiddle, both, band, spread, fan


def pack_width(n):
    return -(-2 * SRC * n // LANES) * LANES


C3 = math.sqrt(3.0) / 2.0
C51, C52 = math.cos(2 * math.pi / 5), math.cos(4 * math.pi / 5)
S51, S52 = math.sin(2 * math.pi / 5), math.sin(4 * math.pi / 5)


def dft3(x0, x1, x2):
    t = x1 + x2
    return x0 + t, x0 - 0.5 * t, C3 * (x2 - x1)


def dft5(x):
    t1, t2 = x[1] + x[4], x[2] + x[3]
    d1, d2 = x[1] - x[4], x[2] - x[3]
    re0 = x[0] + t1 + t2
    re1 = x[0] + C51 * t1 + C52 * t2
    re2 = x[0] + C52 * t1 + C51 * t2
    im1 = -(S51 * d1 + S52 * d2)
    im2 = S51 * d2 - S52 * d1
    return re0, re1, im1, re2, im2


def dft15(x):
    columns = [dft3(*[x[(5 * n1 + 3 * n2) % 15] for n1 in range(3)]) for n2 in range(5)]
    z = dft5([c[0] for c in columns])
    u = dft5([c[1] for c in columns])
    v = dft5([c[2] for c in columns])
    out = {}
    out[(0, 0)] = (z[0], None)
    out[(0, 1)] = (z[1], z[2])
    out[(0, 2)] = (z[3], z[4])
    out[(1, 0)] = (u[0], v[0])
    for j, (b, s) in ((1, (1, 2)), (2, (3, 4))):
        out[(1, j)] = (u[b] - v[s], u[s] + v[b])
        out[(1, 5 - j)] = (u[b] + v[s], v[b] - u[s])
    bins = [None] * 8
    for (k1, k2), (re, im) in out.items():
        k = (10 * k1 + 6 * k2) % 15
        if k <= 7:
            bins[k] = (re, im)
        else:
            bins[15 - k] = (re, -im)
    return bins


def first_stage(rows, base, off, x_ref, twiddle_ref, hi_ref, lo_ref):
    lane = lax.broadcasted_iota(jnp.int32, (16, LANES), 1)
    extra = rows - PARTS

    def put(row, c0, a0, value):
        hi, lo = split(value)
        hi_ref[pl.ds(row * CT + c0, 16), pl.ds(a0, LANES)] = hi
        lo_ref[pl.ds(row * CT + c0, 16), pl.ds(a0, LANES)] = lo

    def block(i, carry):
        c0 = pl.multiple_of(i * 16, 16)

        def load(j):
            return x_ref[pl.ds(base + c0 * rows + j, 16, stride=rows), :]

        for t in range(L // LANES):
            x = []
            for b in range(M):
                j = b * (L // LANES) + t
                value = load(j)
                if j < extra:
                    value = jnp.where(lane + j * LANES < off, load(j + PARTS), value)
                x.append(value)
            bins = dft15(x)
            a0 = t * LANES
            put(14, c0, a0, bins[0][0])
            for r in range(1, 8):
                re, im = bins[r]
                cos = twiddle_ref[2 * r - 2, :, a0 : a0 + LANES]
                sin = twiddle_ref[2 * r - 1, :, a0 : a0 + LANES]
                cos = jnp.concatenate([cos, cos], 0)
                sin = jnp.concatenate([sin, sin], 0)
                put(2 * r - 2, c0, a0, re * cos + im * sin)
                put(2 * r - 1, c0, a0, im * cos - re * sin)
        return carry

    lax.fori_loop(0, CT // 16, block, 0)


def second_stage(both_ref, hi_ref, lo_ref, w_ref):
    nt = (((1,), (1,)), ((), ()))
    low = lax.broadcasted_iota(jnp.int32, (NQ, LANES), 1) < CT

    def second(row, count):
        window = slice(row * CT, (row + count) * CT)
        p = lax.dot_general(both_ref[...], hi_ref[window, :], nt, preferred_element_type=jnp.float32)
        s = lax.dot_general(both_ref[: 2 * NQ, :], lo_ref[window, :], nt, preferred_element_type=jnp.float32)
        z = p[: 2 * NQ] + p[2 * NQ :] + s
        return z[:NQ], z[NQ:]

    for pair in range(4):
        zc, zs = second(4 * pair, min(4, M - 4 * pair))
        for i in range(2):
            r = 2 * pair + 1 + i
            if r == 8:
                w_ref[pl.ds(START, NQ, stride=M), :] = jnp.concatenate([zc[:, LANES:], -zs[:, LANES:]], 1)
                continue
            c = zc[:, i * LANES : (i + 1) * LANES]
            s = pltpu.roll(zs[:, i * LANES : (i + 1) * LANES], CT, 1)
            w_ref[pl.ds(START + r, NQ, stride=M), :] = c + jnp.where(low, s, -s)
            w_ref[pl.ds(START - r, NQ, stride=M), :] = jnp.where(low, c, -c) - s


def normalised(band_ref, w_ref):
    spec = w_ref[BASE : BASE + FB, :]
    power = spec * spec
    amp = jnp.sqrt(power + pltpu.roll(power, CT, 1))
    high = amp.astype(jnp.bfloat16).astype(jnp.float32)
    low = lax.broadcasted_iota(jnp.int32, (FB, LANES), 1) < CT
    parts = jnp.where(low, high, amp - high).astype(jnp.bfloat16)
    total = jnp.dot(band_ref[...], parts, preferred_element_type=jnp.float32)
    total = total + pltpu.roll(total, CT, 1)
    k = lax.broadcasted_iota(jnp.int32, (FB, LANES), 0)
    count = jnp.minimum(k + SMOOTH, FB - 1) - jnp.maximum(k - SMOOTH, 0) + 1
    count = count.astype(jnp.float32)
    return spec * (count / (total + 1e-06 * count))


def kernel(n, nc, rows, nt, off_ref, x_hbm, tw_hbm, both_hbm, band_hbm, spread_hbm, fan_hbm, o_ref,
           x_ref, tw_ref, both_ref, band_ref, spread_ref, fan_ref, hi_ref, lo_ref, w_ref, white, recv,
           src_send, src_recv, b_ref, a_ref,
           x_sem, const_sem, send_sem, recv_sem, ssend_sem, srecv_sem):
    me = lax.axis_index("tm")
    blk = lax.axis_index("chan")
    bins = FB // n
    nsub = bins // KB
    off = off_ref[0]

    def fetch(t):
        part = pl.ds(t * CT * rows, CT * rows)
        return pltpu.make_async_copy(x_hbm.at[part, :], x_ref.at[part, :], x_sem.at[t])

    pairs = ((tw_hbm, tw_ref), (both_hbm, both_ref), (band_hbm, band_ref), (spread_hbm, spread_ref), (fan_hbm, fan_ref))
    consts = [pltpu.make_async_copy(src, dst, const_sem.at[i]) for i, (src, dst) in enumerate(pairs)]
    fetch(0).start()
    for c in consts[:3]:
        c.start()
    for t in range(1, nt):
        fetch(t).start()
    for c in consts[3:]:
        c.start()

    barrier = pltpu.get_barrier_semaphore()
    chan_steps = sorted({s % nc for r in range(1, ROUNDS + 1) for s in (r, -r)} - {0})
    for sh in range(1, n):
        pl.semaphore_signal(barrier, inc=1, device_id={"tm": lax.rem(me + sh, n)}, device_id_type=MESH)
    for s in chan_steps:
        pl.semaphore_signal(barrier, inc=1, device_id={"chan": lax.rem(blk + s, nc)}, device_id_type=MESH)

    def exchange(t, j, sh):
        peer = lax.rem(me + sh, n)
        return pltpu.make_async_remote_copy(
            src_ref=white.at[t, pl.ds(pl.multiple_of(peer * bins + j * KB, 8), KB), :],
            dst_ref=recv.at[sh - 1, t, pl.ds(pl.multiple_of(j * KB, 8), KB), :],
            send_sem=send_sem.at[t, sh - 1, j],
            recv_sem=recv_sem.at[t, sh - 1, j],
            device_id={"tm": peer},
            device_id_type=MESH,
        )

    order = list(range(2, n)) + [1]

    def transform(t, carry):
        fetch(t).wait()

        @pl.when(t == 0)
        def _():
            consts[0].wait()

        first_stage(rows, t * CT * rows, off, x_ref, tw_ref, hi_ref, lo_ref)

        @pl.when(t == 0)
        def _():
            consts[1].wait()

        second_stage(both_ref, hi_ref, lo_ref, w_ref)

        @pl.when(t == 0)
        def _():
            consts[2].wait()

        white[t] = normalised(band_ref, w_ref)

        @pl.when(t == 0)
        def _():
            pl.semaphore_wait(barrier, n - 1 + len(chan_steps))

        for j in range(nsub):
            for sh in order:
                exchange(t, j, sh).start()
        return carry

    lax.fori_loop(0, nt, transform, 0)

    mine = pl.multiple_of(me * bins, 8)
    for j in range(nsub):
        for sh in order:
            exchange(0, j, sh).wait_recv()
    lane = lax.broadcasted_iota(jnp.int32, (bins, LANES), 1)
    for tile in range(src_send.shape[1] // LANES):
        packed = jnp.zeros((bins, LANES), jnp.float32)
        for sh in range(n):
            at = sh * 2 * SRC - tile * LANES
            if not 0 <= at < LANES:
                continue
            value = white[0, pl.ds(mine, bins), :] if sh == 0 else recv[sh - 1, 0]
            re = pltpu.roll(value, at, 1) if at else value
            im = pltpu.roll(value, (at + SRC - CT) % LANES, 1)
            packed = jnp.where((lane >= at) & (lane < at + SRC), re, packed)
            packed = jnp.where((lane >= at + SRC) & (lane < at + 2 * SRC), im, packed)
        src_send[:, tile * LANES : (tile + 1) * LANES] = packed

    def source(r):
        return pltpu.make_async_remote_copy(
            src_ref=src_send,
            dst_ref=src_recv.at[r - 1],
            send_sem=ssend_sem.at[r - 1],
            recv_sem=srecv_sem.at[r - 1],
            device_id={"chan": lax.rem(blk + nc - r, nc)},
            device_id_type=MESH,
        )

    for r in range(1, ROUNDS + 1):
        source(r).start()
    for c in consts[3:]:
        c.wait()
    for r in range(1, ROUNDS + 1):
        source(r).wait_recv()
        b_ref[r - 1] = jnp.dot(twice(src_recv[r - 1]), fan_ref[...], preferred_element_type=jnp.float32) * (1.0 / n)

    def pairing(u, carry):
        t = lax.div(u, nsub)
        j = lax.rem(u, nsub)

        @pl.when(t > 0)
        def _():
            for sh in order:
                exchange(t, j, sh).wait_recv()

        k0 = pl.multiple_of(j * KB, 8)
        a = [white[t, pl.ds(pl.multiple_of(mine + k0, 8), KB), :]]
        a += [recv[sh - 1, t, pl.ds(k0, KB), :] for sh in range(1, n)]
        a_ref[...] = jnp.dot(twice(jnp.concatenate(a, 0)), spread_ref[...], preferred_element_type=jnp.float32)

        def group(g, carry):
            g8 = pl.multiple_of(g * 8, 8)
            b = [[[b_ref[rnd, pl.ds(pl.multiple_of(k0 + g8, 8), 8), (2 * w + p) * LANES : (2 * w + p + 1) * LANES]
                   for p in range(2)] for w in range(n)] for rnd in range(ROUNDS)]
            for tile in range(WIDE // LANES):
                lanes = slice(tile * LANES, (tile + 1) * LANES)
                far = slice(WIDE + tile * LANES, WIDE + (tile + 1) * LANES)
                ar = [a_ref[pl.ds(w * KB + g8, 8), lanes] for w in range(n)]
                ai = [a_ref[pl.ds(w * KB + g8, 8), far] for w in range(n)]
                for rnd in range(ROUNDS):
                    real = imag = None
                    for w in range(n):
                        br, bi = b[rnd][w]
                        p = ar[w] * br + ai[w] * bi
                        q = ai[w] * br - ar[w] * bi
                        real = p if real is None else real + p
                        imag = q if imag is None else imag + q
                    o_ref[t, rnd, pl.ds(pl.multiple_of(k0 + g8, 8), 8), 0, lanes] = real
                    o_ref[t, rnd, pl.ds(pl.multiple_of(k0 + g8, 8), 8), 1, lanes] = imag
            return carry

        lax.fori_loop(0, KB // 8, group, 0)
        return carry

    lax.fori_loop(0, nt * nsub, pairing, 0)

    for r in range(1, ROUNDS + 1):
        source(r).wait_send()

    def drain(t, carry):
        for j in range(nsub):
            for sh in order:
                exchange(t, j, sh).wait_send()
        return carry

    lax.fori_loop(0, nt, drain, 0)


def write_out(nt, x_ref, o_hbm, sem):
    copies = [
        pltpu.make_async_copy(x_ref.at[t, rnd], o_hbm.at[rnd, :, :, pl.ds(t * WIDE, WIDE)], sem.at[t, rnd])
        for t in range(nt)
        for rnd in range(ROUNDS)
    ]
    for c in copies:
        c.start()
    for c in copies:
        c.wait()


def shards(records, offsets):
    chans = records.shape[0]
    n, nc = lax.axis_size("tm"), lax.axis_size("chan")
    rows = records.shape[2] // LANES
    nt = chans // CT
    bins = FB // n
    nsub = bins // KB
    assert records.shape[1] == 1 and chans % CT == 0 and bins % KB == 0
    flat = records.reshape(chans * rows, LANES)
    consts = [jnp.asarray(c) for c in tables(n)]
    anyspace = pl.BlockSpec(memory_space=pl.ANY)
    f32, bf16 = jnp.float32, jnp.bfloat16
    whole = (nt, ROUNDS, bins, 2, WIDE)
    held = pl.pallas_call(
        functools.partial(kernel, n, nc, rows, nt),
        in_specs=[pl.BlockSpec(memory_space=pltpu.SMEM)] + [anyspace] * 6,
        out_specs=pl.BlockSpec(memory_space=pltpu.VMEM),
        out_shape=pltpu.VMEM(whole, f32),
        scratch_shapes=[
            pltpu.VMEM((chans * rows, LANES), f32),
            *[pltpu.VMEM(c.shape, c.dtype) for c in consts],
            pltpu.VMEM((M * CT, L), bf16),
            pltpu.VMEM((M * CT, L), bf16),
            pltpu.VMEM((ROWS + 8, LANES), f32),
            pltpu.VMEM((nt, FB, LANES), f32),
            pltpu.VMEM((n - 1, nt, bins, LANES), f32),
            pltpu.VMEM((bins, pack_width(n)), f32),
            pltpu.VMEM((ROUNDS, bins, pack_width(n)), f32),
            pltpu.VMEM((ROUNDS, bins, 2 * n * LANES), f32),
            pltpu.VMEM((n * KB, 2 * WIDE), f32),
            pltpu.SemaphoreType.DMA((nt,)),
            pltpu.SemaphoreType.DMA((5,)),
            pltpu.SemaphoreType.DMA((nt, n - 1, nsub)),
            pltpu.SemaphoreType.DMA((nt, n - 1, nsub)),
            pltpu.SemaphoreType.DMA((ROUNDS,)),
            pltpu.SemaphoreType.DMA((ROUNDS,)),
        ],
        compiler_params=pltpu.CompilerParams(
            collective_id=0, has_side_effects=True, vmem_limit_bytes=59000 << 10
        ),
        name="correlate",
    )(offsets, flat, *consts)
    return pl.pallas_call(
        functools.partial(write_out, nt),
        in_specs=[pl.BlockSpec(memory_space=pltpu.VMEM)],
        out_specs=anyspace,
        out_shape=jax.ShapeDtypeStruct((ROUNDS, bins, 2, chans * SRC), f32),
        scratch_shapes=[pltpu.SemaphoreType.DMA((nt, ROUNDS))],
        compiler_params=pltpu.CompilerParams(vmem_limit_bytes=8 << 20),
        name="write",
    )(held)


def solution(mesh):
    return jax.shard_map(
        shards,
        mesh=mesh,
        in_specs=(P("chan", "tm", None), P("tm")),
        out_specs=P(None, "tm", None, "chan"),
        check_vma=False,
    )
```

```python
import functools
import math

import jax
import jax.numpy as jnp
import numpy as np
from jax import lax
from jax.experimental import pallas as pl
from jax.experimental.pallas import tpu as pltpu
from jax.sharding import PartitionSpec as P

MESH = pl.DeviceIdType.MESH
SRC = 8
LEN = 7680
FB = 640
FLO = 64
SMOOTH = 64
ROUNDS = 2
M = 15
L = LEN // M
Q0 = FLO // M
NQ = 48
BASE = 16
START = BASE + M * Q0 - FLO
ROWS = START + M // 2 + M * (NQ - 1) + 5
LANES = 128
PARTS = LEN // LANES
CT = 64
WIDE = CT * SRC
KB = 40
STEP = 2 * SMOOTH
FETCH = 16
LATE = 2


def split(x):
    hi = x.astype(jnp.bfloat16)
    return hi, (x - hi.astype(jnp.float32)).astype(jnp.bfloat16)


def twice(x):
    return jnp.concatenate(split(x), 1)


def tables(n):
    a = np.arange(L)
    q = Q0 + np.arange(NQ)
    angle = 2.0 * math.pi * ((q[:, None] * a[None, :]) % L) / L
    full = np.concatenate([np.cos(angle), np.sin(angle)]).astype(np.float32)
    hi = full.astype(jnp.bfloat16)
    lo = (full - hi.astype(np.float32)).astype(jnp.bfloat16)
    both = np.concatenate([hi, lo])
    r = np.arange(1, M // 2 + 1)
    turn = 2.0 * math.pi * (r[:, None] * a[None, :]) / LEN
    twiddle = np.stack([np.cos(turn), np.sin(turn)], 1).reshape(2 * len(r), L)
    twiddle = np.repeat(twiddle[:, None, :], 8, 1).astype(np.float32)
    k = np.arange(STEP)[:, None]
    col = np.arange(2 * STEP)[None, :]
    band = np.stack([np.abs(k + shift - col) <= SMOOTH for shift in (0, SMOOTH, STEP)]).astype(jnp.bfloat16)
    lane = np.arange(LANES)[:, None]
    col = np.arange(2 * WIDE)[None, :]
    spread = lane == (col // WIDE) * CT + (col % WIDE) // SRC
    spread = np.concatenate([spread, spread]).astype(jnp.bfloat16)
    packed = np.arange(pack_width(n))[:, None]
    col = np.arange(2 * n * LANES)[None, :]
    fan = packed == (col // LANES) * SRC + col % SRC
    fan = np.concatenate([fan, fan]).astype(jnp.bfloat16)
    return twiddle, both, band, spread, fan


def pack_width(n):
    return -(-2 * SRC * n // LANES) * LANES


C3 = math.sqrt(3.0) / 2.0
C51, C52 = math.cos(2 * math.pi / 5), math.cos(4 * math.pi / 5)
S51, S52 = math.sin(2 * math.pi / 5), math.sin(4 * math.pi / 5)


def dft3(x0, x1, x2):
    t = x1 + x2
    return x0 + t, x0 - 0.5 * t, C3 * (x2 - x1)


def dft5(x):
    t1, t2 = x[1] + x[4], x[2] + x[3]
    d1, d2 = x[1] - x[4], x[2] - x[3]
    re0 = x[0] + t1 + t2
    re1 = x[0] + C51 * t1 + C52 * t2
    re2 = x[0] + C52 * t1 + C51 * t2
    im1 = -(S51 * d1 + S52 * d2)
    im2 = S51 * d2 - S52 * d1
    return re0, re1, im1, re2, im2


def dft15(x):
    columns = [dft3(*[x[(5 * n1 + 3 * n2) % 15] for n1 in range(3)]) for n2 in range(5)]
    z = dft5([c[0] for c in columns])
    u = dft5([c[1] for c in columns])
    v = dft5([c[2] for c in columns])
    out = {}
    out[(0, 0)] = (z[0], None)
    out[(0, 1)] = (z[1], z[2])
    out[(0, 2)] = (z[3], z[4])
    out[(1, 0)] = (u[0], v[0])
    for j, (b, s) in ((1, (1, 2)), (2, (3, 4))):
        out[(1, j)] = (u[b] - v[s], u[s] + v[b])
        out[(1, 5 - j)] = (u[b] + v[s], v[b] - u[s])
    bins = [None] * 8
    for (k1, k2), (re, im) in out.items():
        k = (10 * k1 + 6 * k2) % 15
        if k <= 7:
            bins[k] = (re, im)
        else:
            bins[15 - k] = (re, -im)
    return bins


def first_stage(rows, chunk, off, arrive, x_ref, twiddle_ref, hi_ref, lo_ref):
    lane = lax.broadcasted_iota(jnp.int32, (16, LANES), 1)
    extra = rows - PARTS

    def put(row, c0, a0, value):
        hi, lo = split(value)
        hi_ref[pl.ds(row * CT + c0, 16), pl.ds(a0, LANES)] = hi
        lo_ref[pl.ds(row * CT + c0, 16), pl.ds(a0, LANES)] = lo

    def block(i, carry):
        c0 = pl.multiple_of(i * FETCH, FETCH)
        piece = chunk * (CT // FETCH) + i
        if arrive is not None:
            arrive(i)

        def load(j):
            return x_ref[pl.ds(piece * FETCH * rows + j, FETCH, stride=rows), :]

        for t in range(L // LANES):
            x = []
            for b in range(M):
                j = b * (L // LANES) + t
                value = load(j)
                if j < extra:
                    value = jnp.where(lane + j * LANES < off, load(j + PARTS), value)
                x.append(value)
            bins = dft15(x)
            a0 = t * LANES
            put(14, c0, a0, bins[0][0])
            for r in range(1, 8):
                re, im = bins[r]
                cos = twiddle_ref[2 * r - 2, :, a0 : a0 + LANES]
                sin = twiddle_ref[2 * r - 1, :, a0 : a0 + LANES]
                cos = jnp.concatenate([cos, cos], 0)
                sin = jnp.concatenate([sin, sin], 0)
                put(2 * r - 2, c0, a0, re * cos + im * sin)
                put(2 * r - 1, c0, a0, im * cos - re * sin)
        return carry

    lax.fori_loop(0, CT // FETCH, block, 0)


def second_stage(both_ref, hi_ref, lo_ref, w_ref):
    nt = (((1,), (1,)), ((), ()))
    low = lax.broadcasted_iota(jnp.int32, (NQ, LANES), 1) < CT

    def second(row, count):
        window = slice(row * CT, (row + count) * CT)
        p = lax.dot_general(both_ref[...], hi_ref[window, :], nt, preferred_element_type=jnp.float32)
        s = lax.dot_general(both_ref[: 2 * NQ, :], lo_ref[window, :], nt, preferred_element_type=jnp.float32)
        z = p[: 2 * NQ] + p[2 * NQ :] + s
        return z[:NQ], z[NQ:]

    for pair in range(4):
        zc, zs = second(4 * pair, min(4, M - 4 * pair))
        for i in range(2):
            r = 2 * pair + 1 + i
            if r == 8:
                w_ref[pl.ds(START, NQ, stride=M), :] = jnp.concatenate([zc[:, LANES:], -zs[:, LANES:]], 1)
                continue
            c = zc[:, i * LANES : (i + 1) * LANES]
            s = pltpu.roll(zs[:, i * LANES : (i + 1) * LANES], CT, 1)
            w_ref[pl.ds(START + r, NQ, stride=M), :] = c + jnp.where(low, s, -s)
            w_ref[pl.ds(START - r, NQ, stride=M), :] = jnp.where(low, c, -c) - s


def normalised(band_ref, w_ref):
    spec = w_ref[BASE : BASE + FB, :]
    power = spec * spec
    amp = jnp.sqrt(power + pltpu.roll(power, CT, 1))
    high = amp.astype(jnp.bfloat16).astype(jnp.float32)
    low = lax.broadcasted_iota(jnp.int32, (FB, LANES), 1) < CT
    parts = jnp.where(low, high, amp - high).astype(jnp.bfloat16)
    total = []
    for i in range(FB // STEP):
        start = min(max(i * STEP - SMOOTH, 0), FB - 2 * STEP)
        window = parts[start : start + 2 * STEP]
        total.append(jnp.dot(band_ref[(i * STEP - start) // SMOOTH], window, preferred_element_type=jnp.float32))
    total = jnp.concatenate(total, 0)
    total = total + pltpu.roll(total, CT, 1)
    k = lax.broadcasted_iota(jnp.int32, (FB, LANES), 0)
    count = jnp.minimum(k + SMOOTH, FB - 1) - jnp.maximum(k - SMOOTH, 0) + 1
    count = count.astype(jnp.float32)
    return spec * (count / (total + 1e-06 * count))


def combine(n, a, k0, a_ref, b_ref, spread_ref, put):
    a_ref[...] = jnp.dot(twice(jnp.concatenate(a, 0)), spread_ref[...], preferred_element_type=jnp.float32)

    def group(g, carry):
        g8 = pl.multiple_of(g * 8, 8)
        b = [[[b_ref[rnd, pl.ds(pl.multiple_of(k0 + g8, 8), 8), (2 * w + p) * LANES : (2 * w + p + 1) * LANES]
               for p in range(2)] for w in range(n)] for rnd in range(ROUNDS)]
        for tile in range(WIDE // LANES):
            lanes = slice(tile * LANES, (tile + 1) * LANES)
            far = slice(WIDE + tile * LANES, WIDE + (tile + 1) * LANES)
            ar = [a_ref[pl.ds(w * KB + g8, 8), lanes] for w in range(n)]
            ai = [a_ref[pl.ds(w * KB + g8, 8), far] for w in range(n)]
            for rnd in range(ROUNDS):
                real = imag = None
                for w in range(n):
                    br, bi = b[rnd][w]
                    p = ar[w] * br + ai[w] * bi
                    q = ai[w] * br - ar[w] * bi
                    real = p if real is None else real + p
                    imag = q if imag is None else imag + q
                put(rnd, g8, 0, lanes, real)
                put(rnd, g8, 1, lanes, imag)
        return carry

    lax.fori_loop(0, KB // 8, group, 0)


def kernel(n, nc, rows, nt, off_hbm, x_hbm, tw_hbm, both_hbm, band_hbm, spread_hbm, fan_hbm,
           o_ref, late_ref, b_ref, spread_ref,
           off_ref, x_ref, tw_ref, both_ref, band_ref, fan_ref, hi_ref, lo_ref, w_ref, white, recv,
           src_send, src_recv, a_ref,
           off_sem, x_sem, const_sem, send_sem, recv_sem, ssend_sem, srecv_sem):
    me = lax.axis_index("tm")
    blk = lax.axis_index("chan")
    bins = FB // n
    nsub = bins // KB

    first = CT // FETCH

    def fetch(start, size, sem):
        part = pl.ds(pl.multiple_of(start * rows, 8), size * rows)
        return pltpu.make_async_copy(x_hbm.at[part, :], x_ref.at[part, :], x_sem.at[sem])

    def piece(i):
        return fetch(i * FETCH, FETCH, i)

    def chunk(t):
        return fetch(t * CT, CT, first - 1 + t)

    pairs = ((tw_hbm, tw_ref), (both_hbm, both_ref), (band_hbm, band_ref), (spread_hbm, spread_ref), (fan_hbm, fan_ref))
    consts = [pltpu.make_async_copy(src, dst, const_sem.at[i]) for i, (src, dst) in enumerate(pairs)]
    shift = pltpu.make_async_copy(off_hbm, off_ref, off_sem.at[0])
    piece(0).start()
    consts[0].start()
    shift.start()
    for i in range(1, first):
        piece(i).start()
    for c in consts[1:3]:
        c.start()
    for t in range(1, nt):
        chunk(t).start()
    for c in consts[3:]:
        c.start()

    barrier = pltpu.get_barrier_semaphore()
    chan_steps = sorted({s % nc for r in range(1, ROUNDS + 1) for s in (r, -r)} - {0})
    for sh in range(1, n):
        pl.semaphore_signal(barrier, inc=1, device_id={"tm": lax.rem(me + sh, n)}, device_id_type=MESH)
    for s in chan_steps:
        pl.semaphore_signal(barrier, inc=1, device_id={"chan": lax.rem(blk + s, nc)}, device_id_type=MESH)

    def exchange(t, part, sh):
        peer = lax.rem(me + sh, n)
        sem, k, size = part
        return pltpu.make_async_remote_copy(
            src_ref=white.at[t, pl.ds(pl.multiple_of(peer * bins + k, 8), size), :],
            dst_ref=recv.at[sh - 1, t, pl.ds(pl.multiple_of(k, 8), size), :],
            send_sem=send_sem.at[t, sh - 1, sem],
            recv_sem=recv_sem.at[t, sh - 1, sem],
            device_id={"tm": peer},
            device_id_type=MESH,
        )

    order = list(range(2, n)) + [1]
    late = late_ref.shape[1]
    early = bins - late
    entire = (0, 0, bins)
    parts = [(j, j * KB, KB) for j in range(early // KB)] + [(early // KB, early, late)]

    def transform(t, arrive):
        first_stage(rows, t, off_ref[0], arrive, x_ref, tw_ref, hi_ref, lo_ref)
        if arrive is not None:
            consts[1].wait()
        second_stage(both_ref, hi_ref, lo_ref, w_ref)
        if arrive is not None:
            consts[2].wait()
        white[t] = normalised(band_ref, w_ref)

    consts[0].wait()
    shift.wait()
    transform(0, lambda i: piece(i).wait())
    pl.semaphore_wait(barrier, n - 1 + len(chan_steps))
    for sh in order:
        exchange(0, entire, sh).start()

    def later(t, carry):
        chunk(t).wait()
        transform(t, None)

        @pl.when(t < nt - 1)
        def _():
            for sh in order:
                exchange(t, entire, sh).start()

        @pl.when(t == nt - 1)
        def _():
            for part in parts:
                for sh in order:
                    exchange(t, part, sh).start()

        return carry

    lax.fori_loop(1, nt, later, 0)

    mine = pl.multiple_of(me * bins, 8)
    for sh in order:
        exchange(0, entire, sh).wait_recv()
    lane = lax.broadcasted_iota(jnp.int32, (bins, LANES), 1)
    for tile in range(src_send.shape[1] // LANES):
        packed = jnp.zeros((bins, LANES), jnp.float32)
        for sh in range(n):
            at = sh * 2 * SRC - tile * LANES
            if not 0 <= at < LANES:
                continue
            value = white[0, pl.ds(mine, bins), :] if sh == 0 else recv[sh - 1, 0]
            re = pltpu.roll(value, at, 1) if at else value
            im = pltpu.roll(value, (at + SRC - CT) % LANES, 1)
            packed = jnp.where((lane >= at) & (lane < at + SRC), re, packed)
            packed = jnp.where((lane >= at + SRC) & (lane < at + 2 * SRC), im, packed)
        src_send[:, tile * LANES : (tile + 1) * LANES] = packed

    def source(r):
        return pltpu.make_async_remote_copy(
            src_ref=src_send,
            dst_ref=src_recv.at[r - 1],
            send_sem=ssend_sem.at[r - 1],
            recv_sem=srecv_sem.at[r - 1],
            device_id={"chan": lax.rem(blk + nc - r, nc)},
            device_id_type=MESH,
        )

    for r in range(1, ROUNDS + 1):
        source(r).start()
    for c in consts[3:]:
        c.wait()
    for r in range(1, ROUNDS + 1):
        source(r).wait_recv()
        b_ref[r - 1] = jnp.dot(twice(src_recv[r - 1]), fan_ref[...], preferred_element_type=jnp.float32) * (1.0 / n)

    def pairing(u, carry):
        t = lax.div(u, nsub)
        j = lax.rem(u, nsub)

        @pl.when((t > 0) & (t < nt - 1) & (j == 0))
        def _():
            for sh in order:
                exchange(t, entire, sh).wait_recv()

        @pl.when(t == nt - 1)
        def _():
            for sh in order:
                exchange(t, (j, j * KB, KB), sh).wait_recv()

        k0 = pl.multiple_of(j * KB, 8)
        a = [white[t, pl.ds(pl.multiple_of(mine + k0, 8), KB), :]]
        a += [recv[sh - 1, t, pl.ds(k0, KB), :] for sh in range(1, n)]

        def put(rnd, k, part, lanes, value):
            o_ref[t, rnd, pl.ds(pl.multiple_of(k0 + k, 8), 8), part, lanes] = value

        combine(n, a, k0, a_ref, b_ref, spread_ref, put)
        return carry

    lax.fori_loop(0, nt * nsub - late // KB, pairing, 0)
    for sh in order:
        exchange(nt - 1, parts[-1], sh).wait_recv()
    late_ref[0] = white[nt - 1, pl.ds(pl.multiple_of(mine + early, 8), late), :]
    for sh in range(1, n):
        late_ref[sh] = recv[sh - 1, nt - 1, early:, :]

    for r in range(1, ROUNDS + 1):
        source(r).wait_send()

    def drain(t, carry):
        for sh in order:
            exchange(t, entire, sh).wait_send()
        return carry

    lax.fori_loop(0, nt - 1, drain, 0)
    for part in parts:
        for sh in order:
            exchange(nt - 1, part, sh).wait_send()


def write_out(n, nt, x_ref, late_ref, b_ref, spread_ref, o_hbm, a_ref, stage, sem, late_sem):
    bins, late = b_ref.shape[1], late_ref.shape[1]
    early = bins - late
    copies = []
    for t in range(nt):
        size = bins if t < nt - 1 else early
        for rnd in range(ROUNDS if size else 0):
            part = pl.ds(0, size)
            to = o_hbm.at[rnd, part, :, pl.ds(t * WIDE, WIDE)]
            copies.append(pltpu.make_async_copy(x_ref.at[t, rnd, part], to, sem.at[t, rnd]))
    for c in copies:
        c.start()
    for j in range(late // KB):
        a = [late_ref[w, j * KB : (j + 1) * KB, :] for w in range(n)]

        def put(rnd, k, part, lanes, value):
            stage[j, rnd, pl.ds(k, 8), part, lanes] = value

        combine(n, a, early + j * KB, a_ref, b_ref, spread_ref, put)
        to = o_hbm.at[:, pl.ds(early + j * KB, KB), :, pl.ds((nt - 1) * WIDE, WIDE)]
        copies.append(pltpu.make_async_copy(stage.at[j], to, late_sem.at[j]))
        copies[-1].start()
    for c in copies:
        c.wait()


def shards(records, offsets):
    chans = records.shape[0]
    n, nc = lax.axis_size("tm"), lax.axis_size("chan")
    rows = records.shape[2] // LANES
    nt = chans // CT
    bins = FB // n
    nsub = bins // KB
    assert records.shape[1] == 1 and chans % CT == 0 and bins % KB == 0 and nt > 1
    flat = records.reshape(chans * rows, LANES)
    consts = [jnp.asarray(c) for c in tables(n)]
    anyspace = pl.BlockSpec(memory_space=pl.ANY)
    f32, bf16 = jnp.float32, jnp.bfloat16
    whole = (nt, ROUNDS, bins, 2, WIDE)
    late = min(LATE, nsub)
    vmem = pl.BlockSpec(memory_space=pltpu.VMEM)
    held = pl.pallas_call(
        functools.partial(kernel, n, nc, rows, nt),
        in_specs=[pl.BlockSpec(memory_space=pltpu.HBM)] + [anyspace] * 6,
        out_specs=[vmem] * 4,
        out_shape=[
            pltpu.VMEM(whole, f32),
            pltpu.VMEM((n, late * KB, LANES), f32),
            pltpu.VMEM((ROUNDS, bins, 2 * n * LANES), f32),
            pltpu.VMEM(consts[3].shape, bf16),
        ],
        scratch_shapes=[
            pltpu.SMEM((1,), jnp.int32),
            pltpu.VMEM((chans * rows, LANES), f32),
            *[pltpu.VMEM(c.shape, c.dtype) for i, c in enumerate(consts) if i != 3],
            pltpu.VMEM((M * CT, L), bf16),
            pltpu.VMEM((M * CT, L), bf16),
            pltpu.VMEM((ROWS + 8, LANES), f32),
            pltpu.VMEM((nt, FB, LANES), f32),
            pltpu.VMEM((n - 1, nt, bins, LANES), f32),
            pltpu.VMEM((bins, pack_width(n)), f32),
            pltpu.VMEM((ROUNDS, bins, pack_width(n)), f32),
            pltpu.VMEM((n * KB, 2 * WIDE), f32),
            pltpu.SemaphoreType.DMA((1,)),
            pltpu.SemaphoreType.DMA((nt + CT // FETCH,)),
            pltpu.SemaphoreType.DMA((5,)),
            pltpu.SemaphoreType.DMA((nt, n - 1, nsub)),
            pltpu.SemaphoreType.DMA((nt, n - 1, nsub)),
            pltpu.SemaphoreType.DMA((ROUNDS,)),
            pltpu.SemaphoreType.DMA((ROUNDS,)),
        ],
        compiler_params=pltpu.CompilerParams(
            collective_id=0, has_side_effects=True, vmem_limit_bytes=57050 << 10
        ),
        name="correlate",
    )(offsets, flat, *consts)
    return pl.pallas_call(
        functools.partial(write_out, n, nt),
        in_specs=[vmem] * 4,
        out_specs=anyspace,
        out_shape=jax.ShapeDtypeStruct((ROUNDS, bins, 2, chans * SRC), f32),
        scratch_shapes=[
            pltpu.VMEM((n * KB, 2 * WIDE), f32),
            pltpu.VMEM((late, ROUNDS, KB, 2, WIDE), f32),
            pltpu.SemaphoreType.DMA((nt, ROUNDS)),
            pltpu.SemaphoreType.DMA((late,)),
        ],
        compiler_params=pltpu.CompilerParams(vmem_limit_bytes=10 << 20),
        name="write",
    )(*held)


def solution(mesh):
    return jax.shard_map(
        shards,
        mesh=mesh,
        in_specs=(P("chan", "tm", None), P("tm")),
        out_specs=P(None, "tm", None, "chan"),
        check_vma=False,
    )
```
